512 devices in a mesh: seq: 64 (over x, y, core), head: 8 (over z).
Axes of the slice: x: 4, y: 8, z: 8, core: 2. Of those that a mesh axis runs over, the one named last changes fastest.
Arguments:
- queries: bfloat16 [69632, 2048], P('seq', 'head'), may hold values from -50 to 50
- keys: bfloat16 [69632, 2048], P('seq', 'head'), may hold values from -6 to 6
- values: bfloat16 [69632, 2048], P('seq', 'head'), may hold values from -48 to 48
- rand_group: int32 [1088, 3], replicated, may hold values from 0 to 63, all different within a row; in each aligned block of 17 rows (0 to 16, 17 to 33, ...) at most 2 rows name the same one
- rand_offset: int32 [1088, 3], replicated, may hold values from 0 to 16
- glob_blocks: int32 [2], replicated, may hold values from 0 to 1087
- w_out: bfloat16 [2048, 4096], P(None, 'head'), may hold values from -0.125 to 0.125
Outputs:
- layer_out: bfloat16 [69632, 4096], P('seq', 'head')
The draws below stay inside these ranges and needn't reach their ends.
Inputs may be any that keep to these rules, and one draw needn't show every extreme that they name: `rand_group`: each row names 3 different groups. Among the 17 rows of one aligned block of 17 rows, no group is named more than 2 times, and in every draw some group is named exactly 2 times in some such block.
All inputs are finite; a program needn't handle non-finite values.
Results may differ from the reference program's by a relative error of at most 0.0056.
Values may be sent and summed in bfloat16 or wider, within the bound.
A program may use at most 128 MiB of HBM per device.

```python
import math
import jax
import jax.numpy as jnp
import numpy as np
from jax import lax

D = 4096
DH = 128
BLOCK = 64
R = 3
G = 2
TOKENS = 69632
NB = 1088
BPD = 17
CAP = 2
HEADS = 16
N_SEQ = 64


def draw_keys(key, part):
    result = jnp.clip(jax.random.normal(jax.random.fold_in(key, 11), (TOKENS, HEADS * DH), jnp.float32), -6.0, 6.0)
    return result.astype(jnp.bfloat16)


def draw_queries(key, part):
    result = jnp.clip(jax.random.normal(jax.random.fold_in(key, 23), (TOKENS, HEADS * DH), jnp.float32), -6.0, 6.0)
    return result.astype(jnp.bfloat16)


def with_ends(entries, key, smallest, largest):
    extent = entries.shape
    index_at = [jax.random.randint(jax.random.fold_in(key, axis), (), 0, extent[axis]) for axis in range(len(extent))]
    entries = entries.at[tuple(index_at)].set(smallest)
    longest = extent.index(max(extent))
    index_at[longest] = (index_at[longest] + 1) % extent[longest]
    return entries.at[tuple(index_at)].set(largest)


def block_levels(own_key, extent, pieces, low, high):
    factor_of, own = 1.0, jax.random.fold_in(own_key, 6)
    for position, shards_of in pieces:
        heights = jnp.exp(jax.random.uniform(jax.random.fold_in(own, position), (shards_of,), jnp.float32, low / len(pieces), high / len(pieces)))
        factor_of = factor_of * jnp.repeat(heights, extent[position] // shards_of).reshape([-1 if axis == position else 1 for axis in range(len(extent))])
    return factor_of


def deal_out(own_key, own, number, rows, amount, top, reach, lean):
    sequence = jax.random.permutation(own_key, amount)
    packed, common = shares(amount, rows * top, reach, lean, True), shares(amount, rows * top, reach, lean, False)
    places = jnp.arange(amount)

    def named(tallies, turn):
        used = int((tallies > 0).sum())
        fixed = max(1, used // 4)
        shifted = fixed + (places - fixed + turn * (used - fixed)) % max(1, amount - fixed)
        return jnp.zeros((amount,), jnp.int32).at[sequence[jnp.where(places < fixed, places, shifted)]].set(jnp.asarray(tallies, jnp.int32))

    tallies = jnp.where(number % 4 == 0, named(packed, number // 4), named(common, number - number // 4 - 1))
    mixed = jax.random.permutation(jax.random.fold_in(own, 3), amount)
    giver, receiver = mixed[0:amount // 2 * 2:2], mixed[1:amount // 2 * 2:2]
    slack = jnp.minimum(tallies[giver] - 1, reach - tallies[receiver]) // 2
    slack = jnp.where((giver == sequence[0]) | (receiver == sequence[0]) | (tallies[receiver] == 0), 0, jnp.maximum(slack, 0))
    shifted = jax.random.randint(jax.random.fold_in(own, 4), (amount // 2,), 0, 1 << 20) % (slack + 1)
    tallies = tallies.at[giver].add(-shifted).at[receiver].add(shifted)
    labels = jnp.searchsorted(jnp.cumsum(tallies), jnp.arange(rows * top), side="right").astype(jnp.int32)
    grid = labels.reshape(top, rows).T
    grid = grid[jax.random.permutation(jax.random.fold_in(own, 1), rows)]
    turn = jax.random.randint(jax.random.fold_in(own, 2), (rows, 1), 0, top)
    return jnp.take_along_axis(grid, (jnp.arange(top)[None, :] + turn) % top, axis=1)


def shares(number_of, total, limit, skew, full):
    weights = [(1 << 20) // math.isqrt(grade ** skew) + 1 for grade in range(1, number_of + 1)]
    largest = limit if full else min(limit, max(-(-total // number_of), total * weights[0] // sum(weights)))
    least = 1 if total - largest >= number_of - 1 else 0
    holding, spare = [largest] + [least] * (number_of - 1), total - largest - least * (number_of - 1)
    while spare > 0:
        free = [i for i in range(1, number_of) if holding[i] < largest] or [i for i in range(1, number_of) if holding[i] < limit]
        whole, left = sum([weights[i] for i in free]), spare
        for i in free:
            extra = min(limit - holding[i], max(1, left * weights[i] // whole), spare)
            holding[i] = holding[i] + extra
            spare = spare - extra
    return np.array(holding)


def noise(stream_key, shape, deviation, limit, pieces=(), kind=jnp.bfloat16):
    values = jax.random.normal(stream_key, shape, jnp.float32) * deviation
    if len(pieces) > 0:
        values = block_levels(stream_key, shape, pieces, -0.22, 0.18) * values
    return jnp.clip(values, min=-limit, max=limit).astype(kind)


def setup_inputs(seed: int = 0) -> dict:
    seeds = jax.random.split(jax.random.key(seed), 8)
    queries = draw_queries(jax.random.fold_in(seeds[7], 71), 0)
    keys = draw_keys(jax.random.fold_in(seeds[7], 71), 0)
    values = noise(seeds[2], (TOKENS, HEADS * DH), 8.0, 48.0, ((0, 64), (1, 8)))
    rand_group_keys = jax.random.split(jax.random.fold_in(seeds[3], 1), NB // BPD)
    rand_group_turns = jax.random.permutation(jax.random.fold_in(seeds[3], 3), NB // BPD)
    rand_group = jax.vmap(lambda own, number: deal_out(jax.random.fold_in(seeds[3], 2), own, number, BPD, N_SEQ, R, CAP, 2))(rand_group_keys, rand_group_turns).reshape((NB, R))
    rand_offset = with_ends(jax.random.randint(seeds[4], (NB, R), 0, BPD), jax.random.fold_in(seeds[4], 1), 0, BPD - 1).astype(jnp.int32)
    glob_blocks = jax.random.randint(seeds[5], (G,), 0, NB).astype(jnp.int32)
    w_out = noise(seeds[6], (HEADS * DH, D), (HEADS * DH) ** -0.5, 0.125, ((1, 8),))
    return {"queries": queries, "keys": keys, "values": values, "rand_group": rand_group, "rand_offset": rand_offset, "glob_blocks": glob_blocks, "w_out": w_out}


def attend_blocks(query_rows, key_rows, value_rows):
    score_scale = 1.0 / math.sqrt(DH)
    scores = jnp.einsum('nqhd,nkhd->nhqk', query_rows.astype(jnp.float32), key_rows.astype(jnp.float32)) * score_scale
    row_max = lax.optimization_barrier(jnp.max(scores, axis=-1, keepdims=True))
    weights = jnp.exp(scores - row_max)
    row_total = lax.optimization_barrier(jnp.sum(weights, axis=-1))
    probs = lax.optimization_barrier(weights.astype(jnp.bfloat16))
    weighted = jnp.einsum('nhqk,nkhd->nqhd', probs.astype(jnp.float32), value_rows.astype(jnp.float32))
    return (weighted / jnp.transpose(row_total, (0, 2, 1))[..., None]).astype(jnp.bfloat16)

def reference(queries, keys, values, rand_group, rand_offset, glob_blocks, w_out):
    columns = HEADS * DH
    block_count = TOKENS // BLOCK
    pair_blocks = jnp.concatenate([keys, values], axis=1).reshape(block_count, BLOCK, 2 * columns)
    query_blocks = queries.reshape(block_count, BLOCK, HEADS, DH)
    block_index = jnp.arange(block_count, dtype=jnp.int32)
    window_ids = jnp.stack([(block_index - 1) % block_count, block_index, (block_index + 1) % block_count], axis=1)
    global_ids = jnp.broadcast_to(glob_blocks[None, :].astype(jnp.int32), (block_count, G))
    random_ids = (rand_group * BPD + rand_offset).astype(jnp.int32)
    key_ids = jnp.concatenate([window_ids, global_ids, random_ids], axis=1).astype(jnp.int32)
    group_count = block_count // BPD

    def one_group(group_index):
        first_block = (group_index * BPD).astype(jnp.int32)
        chosen_ids = lax.dynamic_slice_in_dim(key_ids, first_block, BPD, 0)
        gathered = jnp.take(pair_blocks, chosen_ids.reshape(-1), axis=0).reshape(BPD, -1, 2 * columns)
        key_rows = gathered[..., :columns].reshape(BPD, -1, HEADS, DH)
        value_rows = gathered[..., columns:].reshape(BPD, -1, HEADS, DH)
        query_rows = lax.dynamic_slice_in_dim(query_blocks, first_block, BPD, 0)
        return attend_blocks(query_rows, key_rows, value_rows)
    context = lax.map(one_group, jnp.arange(group_count, dtype=jnp.int32)).reshape(TOKENS, columns)
    return jnp.dot(context, w_out, preferred_element_type=jnp.float32).astype(jnp.bfloat16)
```

```python
import math

import jax
import jax.numpy as jnp
from jax import lax
from jax.experimental import pallas as pl
from jax.experimental.pallas import tpu as pltpu
from jax.sharding import PartitionSpec as P

MESH = pl.DeviceIdType.MESH
DH = 128
BLOCK = 64
R = 3
G = 2
NX, NY, NC, NZ = 4, 8, 2, 8
PER = 17
HEADS = 2
COLS = NX * NC
SLOTS = 2 * NY + G
KEYS = 8 * BLOCK
CUT = 9
PIECES = ((0, CUT), (CUT, PER - CUT))
SCALE = 1.0 / math.sqrt(DH)
STEP_KS = ((0,), (1, 2), (3, 4), (5, 6), (7,))
Y_OF_K = (0, -1, 1, -2, 2, -3, 3, 4)
K_OF_DY = (0, 2, 4, 6, 7, 5, 3, 1)
TILE = 272


def place():
    seq = lax.axis_index("seq")
    return seq // (NY * NC), (seq // NC) % NY, seq % NC, lax.axis_index("head")


def exchange_tables(rand_group, rand_offset, glob_blocks):
    x, y, c, _ = place()
    seq = lax.axis_index("seq")
    count = PER * R
    code = (rand_group * 32 + rand_offset).reshape(NX, NY, NC * count)
    row = lax.dynamic_index_in_dim(code, y, 1, keepdims=False).reshape(COLS, count)
    j = jnp.arange(COLS, dtype=jnp.int32)
    receiver = ((x - j // NC) % NX) * NC + (c - j % NC) % NC
    row = jnp.take(row, receiver, axis=0)
    ys = (y + jnp.array(Y_OF_K, jnp.int32)) % NY
    groups = (x * NY + ys) * NC + c
    match = (row // 32)[:, None, :] == groups[None, :, None]
    ranked = jnp.arange(count, dtype=jnp.int32)[None, :] * 32 + row % 32
    ranked = ranked[:, None, :]
    first = jnp.min(jnp.where(match, ranked, 1 << 12), axis=2) % 32
    last = jnp.max(jnp.where(match, ranked, 0), axis=2) % 32
    send = jnp.stack([first, last], axis=2).reshape(-1)

    k_of_dy = jnp.array(K_OF_DY, jnp.int32)

    def column(group):
        return ((group // (NY * NC) - x) % NX) * NC + (group % NC - c) % NC

    def ring(group):
        dy = ((group // NC) % NY - y) % NY
        return jnp.sum(jnp.where(dy[..., None] == jnp.arange(NY), k_of_dy, 0), axis=-1)

    mine = lax.dynamic_slice_in_dim(rand_group, seq * PER, PER, 0).reshape(-1)
    n = jnp.arange(count, dtype=jnp.int32)
    earlier = (mine[:, None] == mine[None, :]) & (n[None, :] < n[:, None])
    rank = jnp.sum(earlier.astype(jnp.int32), axis=1)
    rand_slots = (column(mine) * SLOTS + 2 * ring(mine) + rank).reshape(PER, R)
    glob_group = glob_blocks // PER
    glob_slots = column(glob_group) * SLOTS + 2 * NY + jnp.arange(G, dtype=jnp.int32)
    read = jnp.concatenate([jnp.broadcast_to(glob_slots[None], (PER, G)), rand_slots], axis=1).reshape(-1)
    cand = jnp.stack([ring(glob_group), glob_blocks % PER], axis=1).reshape(-1)
    return send.astype(jnp.int32), read.astype(jnp.int32), cand.astype(jnp.int32)


def kernel(*refs):
    send_t, read_t, cand_t, q_ref, k_ref, v_ref, w_ref, out_ref, *refs = refs
    y_bufs = [refs[7 * sl : 7 * sl + 7] for sl in range(4)]
    refs = refs[28:]
    stage, land, pads = refs[0:4], refs[4:8], refs[8:12]
    p_bufs, t_bufs, ctx, w_bufs = refs[12:14], refs[14:16], refs[16:18], refs[18:20]
    acc, y_s, y_r, x_s, x_r, h_s, h_r, z_s, z_r, w_s = refs[20:]
    x, y, c, z = place()

    def dev(dx=0, dy=0, dc=0, dz=0):
        return (((x + dx) % NX * NY + (y + dy) % NY) * NC + (c + dc) % NC, (z + dz) % NZ)

    seq = lax.axis_index("seq")
    n_seq = NX * NY * NC
    ahead, behind = ((seq + 1) % n_seq, z), ((seq + n_seq - 1) % n_seq, z)
    y_up, y_down, z_up, z_down = dev(dy=1), dev(dy=NY - 1), dev(dz=1), dev(dz=NZ - 1)
    row = [None] + [dev(dx=NX - j // NC, dc=NC - j % NC) for j in range(1, COLS)]
    order = (4, 5, 2, 3, 6, 7, 1)

    def remote(src, dst, s, r, to):
        return pltpu.make_async_remote_copy(
            src_ref=src, dst_ref=dst, send_sem=s, recv_sem=r, device_id=to, device_id_type=MESH
        )

    peers = [y_up, y_down, z_up, z_down, ahead, behind] + row[1:]
    barrier = pltpu.get_barrier_semaphore()
    for peer in peers:
        pl.semaphore_signal(barrier, inc=1, device_id=peer, device_id_type=MESH)

    w_copies = []
    for h in range(HEADS):
        for k in range(NZ):
            rows = ((z + Y_OF_K[k] + NZ) % NZ * HEADS + h) * DH
            copy = pltpu.make_async_copy(
                w_ref.at[pl.ds(pl.multiple_of(rows, DH), DH)], w_bufs[h].at[pl.ds(k * DH, DH)], w_s.at[h * NZ + k]
            )
            copy.start()
            w_copies.append(copy)

    pl.semaphore_wait(barrier, len(peers))

    def own(sl):
        ref = k_ref if sl < 2 else v_ref
        cols = pl.ds(sl % 2 * DH, DH)
        return ref, cols

    pending = []

    def y_copy(sl, step, up, piece):
        start, size = PIECES[piece]
        blocks = pl.ds(start, size)
        if step == 1:
            ref, cols = own(sl)
            src = ref.at[blocks, :, cols]
        else:
            src = y_bufs[sl][2 * step - (4 if up else 3)].at[blocks]
        dst = y_bufs[sl][6 if step == 4 else 2 * step - (2 if up else 1)].at[blocks]
        n = (step - 1) * 4 + (0 if up else 2) + piece
        return remote(src, dst, y_s.at[sl, n], y_r.at[sl, n], y_up if up else y_down)

    def y_send(sl, step, up, piece):
        if step == 4 and up != (piece == 0):
            return
        copy = y_copy(sl, step, up, piece)
        copy.start()
        pending.append(copy)

    def y_begin(sl):
        for piece in (0, 1):
            for up in (True, False):
                y_send(sl, 1, up, piece)

    def y_step(sl, step):
        for piece in (0, 1):
            for up in (True, False):
                if step == 4 and up != (piece == 0):
                    continue
                y_copy(sl, step, up, piece).wait_recv()
                if step < 4:
                    y_send(sl, step + 1, up, piece)

    def load(sl, k, off):
        if k == 0:
            ref, cols = own(sl)
            return ref[off, :, cols]
        return y_bufs[sl][k - 1][off]

    def x_step(sl, step):
        ks = STEP_KS[step]

        def fill(j, _):
            for k in ks:
                for slot in range(2):
                    off = send_t[j * 2 * NY + 2 * k + slot]
                    stage[sl][(j - 1) * SLOTS + 2 * k + slot] = load(sl, k, off)
            return 0

        lax.fori_loop(1, COLS, fill, 0)
        first, size = 2 * ks[0], 2 * len(ks)
        if step == 4:
            size += G
            for g in range(G):
                at = cand_t[2 * g]
                off = cand_t[2 * g + 1]
                block = load(sl, 0, off)
                for k in range(1, NY):
                    block = jnp.where(at == k, load(sl, k, off), block)
                land[sl][2 * NY + g] = block
                for j in range(1, COLS):
                    stage[sl][(j - 1) * SLOTS + 2 * NY + g] = block
        for j in order:
            remote(
                stage[sl].at[pl.ds((j - 1) * SLOTS + first, size)],
                land[sl].at[pl.ds(j * SLOTS + first, size)],
                x_s.at[sl],
                x_r.at[sl],
                row[j],
            ).start()
        for k in ks:
            for slot in range(2):
                land[sl][2 * k + slot] = load(sl, k, send_t[2 * k + slot])

    def x_whole(sl):
        return remote(
            stage[sl].at[...], land[sl].at[pl.ds(SLOTS, (COLS - 1) * SLOTS)], x_s.at[sl], x_r.at[sl], row[1]
        )

    halo = []

    def edges(sl):
        ref, cols = own(sl)
        for n, (src, dst, to) in enumerate(((PER - 1, 0, ahead), (0, PER + 1, behind))):
            copy = remote(ref.at[src, :, cols], pads[sl].at[dst], h_s.at[sl, n], h_r.at[sl, n], to)
            copy.start()
            halo.append(copy)

        def fill(i, _):
            pads[sl][i + 1] = ref[i, :, cols]
            return 0

        lax.fori_loop(0, PER, fill, 0)

    def edges_wait(sl):
        for n in range(2):
            halo[2 * sl + n].wait_recv()

    def gathered(sl, i):
        return jnp.concatenate(
            [pads[sl][i], pads[sl][i + 1], pads[sl][i + 2]]
            + [land[sl][read_t[(G + R) * i + n]] for n in range(G + R)],
            axis=0,
        )

    def scores(h, start, stop):
        def one(i, _):
            s = lax.dot_general(
                q_ref[i, :, pl.ds(h * DH, DH)],
                gathered(h, i),
                (((1,), (1,)), ((), ())),
                preferred_element_type=jnp.float32,
            )
            s = s * SCALE
            e = jnp.exp(s - jnp.max(s, axis=1, keepdims=True))
            t_bufs[h][i] = jnp.broadcast_to(jnp.sum(e, axis=1, keepdims=True), (BLOCK, DH))
            p_bufs[h][i] = e.astype(jnp.bfloat16)
            return 0

        lax.fori_loop(start, stop, one, 0)

    def context(h, start, stop):
        def one(i, _):
            o = jnp.dot(p_bufs[h][i], gathered(2 + h, i), preferred_element_type=jnp.float32)
            rows = pl.ds(pl.multiple_of(i * BLOCK, BLOCK), BLOCK)
            ctx[h][rows, pl.ds(0, DH)] = (o / t_bufs[h][i]).astype(jnp.bfloat16)
            return 0

        lax.fori_loop(start, stop, one, 0)

    ROWS = PER * BLOCK
    Z_PIECES = ((0, CUT * BLOCK), (CUT * BLOCK, ROWS - CUT * BLOCK))

    def z_copy(h, step, up, piece):
        rows = pl.ds(*Z_PIECES[piece])
        from_k = 0 if step == 1 else 2 * step - (3 if up else 2)
        to_k = 7 if step == 4 else 2 * step - (1 if up else 0)
        n = (step - 1) * 4 + (0 if up else 2) + piece
        return remote(
            ctx[h].at[rows, pl.ds(from_k * DH, DH)],
            ctx[h].at[rows, pl.ds(to_k * DH, DH)],
            z_s.at[h, n],
            z_r.at[h, n],
            z_up if up else z_down,
        )

    def z_send(h, step, up, piece):
        if step == 4 and up != (piece == 0):
            return
        copy = z_copy(h, step, up, piece)
        copy.start()
        pending.append(copy)

    def z_begin(h, piece):
        for up in (True, False):
            z_send(h, 1, up, piece)

    def z_step(h, step):
        for piece in (0, 1):
            for up in (True, False):
                if step == 4 and up != (piece == 0):
                    continue
                z_copy(h, step, up, piece).wait_recv()
                if step < 4:
                    z_send(h, step + 1, up, piece)

    def project(h, k0, k1, first=False, last=False):
        cols = pl.ds(k0 * DH, (k1 - k0) * DH)

        def tile(n, _):
            rows = pl.ds(pl.multiple_of(n * TILE, 16), TILE)
            part = jnp.dot(ctx[h][rows, cols], w_bufs[h][cols, :], preferred_element_type=jnp.float32)
            if not first:
                part = part + acc[rows, :]
            if last:
                out_ref[rows, :] = part.astype(out_ref.dtype)
            else:
                acc[rows, :] = part
            return 0

        lax.fori_loop(0, ROWS // TILE, tile, 0)

    y_begin(0)
    for sl in range(2):
        edges(sl)
    x_step(0, 0)

    y_step(0, 1)
    x_step(0, 1)
    edges(2)
    y_step(0, 2)
    x_step(0, 2)
    edges(3)
    y_step(0, 3)
    y_begin(1)
    x_step(0, 3)
    y_step(0, 4)
    x_step(0, 4)
    x_step(1, 0)

    y_step(1, 1)
    x_step(1, 1)
    y_step(1, 2)
    x_step(1, 2)
    edges_wait(0)
    x_whole(0).wait_recv()
    scores(0, 0, 4)
    y_step(1, 3)
    y_begin(2)
    x_step(1, 3)
    scores(0, 4, 9)
    y_step(1, 4)
    x_step(1, 4)
    x_step(2, 0)
    scores(0, 9, 13)

    y_step(2, 1)
    x_step(2, 1)
    scores(0, 13, 17)
    y_step(2, 2)
    x_step(2, 2)
    edges_wait(1)
    x_whole(1).wait_recv()
    scores(1, 0, 4)
    y_step(2, 3)
    y_begin(3)
    x_step(2, 3)
    scores(1, 4, 9)
    y_step(2, 4)
    x_step(2, 4)
    x_step(3, 0)
    scores(1, 9, 13)

    y_step(3, 1)
    x_step(3, 1)
    scores(1, 13, 17)
    edges_wait(2)
    edges_wait(3)
    y_step(3, 2)
    x_step(3, 2)
    x_whole(2).wait_recv()
    context(0, 0, CUT)
    z_begin(0, 0)
    context(0, CUT, PER)
    z_begin(0, 1)
    y_step(3, 3)
    x_step(3, 3)
    z_step(0, 1)
    y_step(3, 4)
    x_step(3, 4)
    z_step(0, 2)
    x_whole(3).wait_recv()
    context(1, 0, CUT)
    z_begin(1, 0)
    context(1, CUT, PER)
    z_begin(1, 1)
    z_step(0, 3)
    for copy in w_copies:
        copy.wait()
    z_step(0, 4)
    z_step(1, 1)
    project(0, 0, 8, first=True)
    z_step(1, 2)
    project(1, 0, 4)
    z_step(1, 3)
    project(1, 4, 6)
    z_step(1, 4)
    project(1, 6, 8, last=True)

    for copy in pending:
        copy.wait_send()
    for copy in halo:
        copy.wait_send()
    for sl in range(4):
        x_whole(sl).wait_send()


def on_device(queries, keys, values, rand_group, rand_offset, glob_blocks, w_out):
    tables = exchange_tables(rand_group, rand_offset, glob_blocks)
    shape = (PER, BLOCK, HEADS * DH)
    bf16 = jnp.bfloat16
    group = pltpu.VMEM((PER, BLOCK, DH), bf16)
    scratch = [group] * 28
    scratch += [pltpu.VMEM(((COLS - 1) * SLOTS, BLOCK, DH), bf16)] * 4
    scratch += [pltpu.VMEM((COLS * SLOTS, BLOCK, DH), bf16)] * 4
    scratch += [pltpu.VMEM((PER + 2, BLOCK, DH), bf16)] * 4
    scratch += [pltpu.VMEM((PER, BLOCK, KEYS), bf16)] * 2
    scratch += [pltpu.VMEM((PER, BLOCK, DH), jnp.float32)] * 2
    scratch += [pltpu.VMEM((PER * BLOCK, NZ * DH), bf16)] * 2
    scratch += [pltpu.VMEM((NZ * DH, w_out.shape[1]), bf16)] * 2
    scratch += [pltpu.VMEM((PER * BLOCK, w_out.shape[1]), jnp.float32)]
    dma = pltpu.SemaphoreType.DMA
    scratch += [dma((4, 16)), dma((4, 16)), dma((4,)), dma((4,)), dma((4, 2)), dma((4, 2))]
    scratch += [dma((2, 16)), dma((2, 16)), dma((2 * NZ,))]
    smem = pl.BlockSpec(memory_space=pltpu.SMEM)
    vmem = pl.BlockSpec(memory_space=pltpu.VMEM)
    return pl.pallas_call(
        kernel,
        out_shape=jax.ShapeDtypeStruct((PER * BLOCK, w_out.shape[1]), bf16),
        in_specs=[smem, smem, smem, vmem, vmem, vmem, pl.BlockSpec(memory_space=pl.ANY)],
        out_specs=vmem,
        scratch_shapes=scratch,
        compiler_params=pltpu.CompilerParams(collective_id=0, has_side_effects=True, vmem_limit_bytes=60 << 20),
        name="sparse_attention",
    )(*tables, queries.reshape(shape), keys.reshape(shape), values.reshape(shape), w_out)


def solution(mesh):
    return jax.shard_map(
        on_device,
        mesh=mesh,
        in_specs=(P("seq", "head"), P("seq", "head"), P("seq", "head"), P(), P(), P(), P(None, "head")),
        out_specs=P("seq", "head"),
        check_vma=False,
    )
```

```python
import math

import jax
import jax.numpy as jnp
from jax import lax
from jax.experimental import pallas as pl
from jax.experimental.pallas import tpu as pltpu
from jax.sharding import PartitionSpec as P

MESH = pl.DeviceIdType.MESH
DH = 128
BLOCK = 64
HALF = 32
R = 3
G = 2
NX, NY, NC, NZ = 4, 8, 2, 8
PER = 17
ROWS = PER * BLOCK
HEADS = 2
COLS = NX * NC
SLOTS = 2 * NY
KEYS = 8 * BLOCK
CUT = 9
PIECES = ((0, CUT), (CUT, PER - CUT))
SCALE = 1.0 / math.sqrt(DH)
STEP_KS = ((0,), (1, 2), (3, 4), (5, 6), (7,))
Y_OF_K = (0, -1, 1, -2, 2, -3, 3, 4)
K0, V0, K1, V1A, V1B = range(5)
HEIGHT = (BLOCK, BLOCK, BLOCK, HALF, HALF)
TILE = 272
BF16 = jnp.bfloat16


def place():
    seq = lax.axis_index("seq")
    return seq // (NY * NC), (seq // NC) % NY, seq % NC, lax.axis_index("head")


def kernel(*refs):
    glob, code_ref, q_hbm, k_hbm, v_hbm, w_ref, out_ref, *refs = refs
    q_ref, k_ref, v_ref, send_v, read_v, send_t, read_t, *refs = refs
    y_bufs = [refs[7 * sl : 7 * sl + 7] for sl in range(5)]
    refs = refs[35:]
    stage, land, pads, g_out, g_in, g_sel, g_other, g_fin = [refs[5 * n : 5 * n + 5] for n in range(8)]
    refs = refs[40:]
    packed, p_bufs, t_bufs, ctx, w_hi, refs = refs[0:2], refs[2:4], refs[4:6], refs[6:9], refs[9:11], refs[11:]
    w_lo, refs = refs[0:3], refs[3:]
    acc, y_s, y_r, x_s, x_r, g_s, g_r, c_s, c_r, h_s, h_r, z_s, z_r, w_s, i_s = refs
    x, y, c, z = place()
    seq = lax.axis_index("seq")

    def dev(dx=0, dy=0, dc=0, dz=0):
        return (((x + dx) % NX * NY + (y + dy) % NY) * NC + (c + dc) % NC, (z + dz) % NZ)

    n_seq = NX * NY * NC
    ahead, behind = ((seq + 1) % n_seq, z), ((seq + n_seq - 1) % n_seq, z)
    y_up, y_down, z_up, z_down = dev(dy=1), dev(dy=NY - 1), dev(dz=1), dev(dz=NZ - 1)
    row = [dev(dx=NX - j // NC, dc=NC - j % NC) for j in range(COLS)]
    order = (4, 5, 2, 3, 6, 7, 1)

    def remote(src, dst, s, r, to):
        return pltpu.make_async_remote_copy(
            src_ref=src, dst_ref=dst, send_sem=s, recv_sem=r, device_id=to, device_id_type=MESH
        )

    peers = [y_up, y_down, z_up, z_down, ahead, behind] + row[1:]
    barrier = pltpu.get_barrier_semaphore()
    for peer in peers:
        pl.semaphore_signal(barrier, inc=1, device_id=peer, device_id_type=MESH)

    in_copies = [
        pltpu.make_async_copy(src, dst, i_s.at[n])
        for n, (src, dst) in enumerate(((k_hbm, k_ref), (v_hbm, v_ref), (q_hbm, q_ref)))
    ]
    for copy in in_copies:
        copy.start()

    w_copies = []

    def w_copy(start, size, dst):
        copy = pltpu.make_async_copy(w_ref.at[pl.ds(pl.multiple_of(start, HALF), size)], dst, w_s.at[len(w_copies)])
        copy.start()
        w_copies.append(copy)

    def w_begin():
        for k in range(NZ):
            at = (z + Y_OF_K[k] + NZ) % NZ * (HEADS * DH)
            w_copy(at, DH, w_lo[0].at[pl.ds(k * DH, DH)])
            for a in range(2):
                w_copy(at + DH + a * BLOCK, BLOCK, w_lo[1 + a].at[pl.ds(k * DH, BLOCK)])
                w_copy(at + DH + a * BLOCK, BLOCK, w_hi[a].at[pl.ds(k * DH + BLOCK, BLOCK)])

    def w_zeros():
        zeros = jnp.zeros((BLOCK, w_ref.shape[1]), BF16)
        for a in range(2):
            for k in range(NZ):
                w_lo[1 + a][pl.ds(k * DH + BLOCK, BLOCK), :] = zeros
                w_hi[a][pl.ds(k * DH, BLOCK), :] = zeros

    in_copies[0].wait()
    pl.semaphore_wait(barrier, len(peers))

    def source(sl, blocks):
        if sl in (K0, K1):
            return k_ref.at[blocks, :, pl.ds(DH if sl == K1 else 0, DH)]
        if sl == V0:
            return v_ref.at[blocks, :, pl.ds(0, DH)]
        return packed[sl - V1A].at[blocks]

    def load(sl, k, off):
        if k:
            return y_bufs[sl][k - 1][off]
        if sl in (K0, K1):
            return k_ref[off, :, pl.ds(DH if sl == K1 else 0, DH)]
        if sl == V0:
            return v_ref[off, :, pl.ds(0, DH)]
        return packed[sl - V1A][off]

    pending = []

    def start(copy):
        copy.start()
        pending.append(copy)

    def y_copy(sl, step, up, piece):
        blocks = pl.ds(*PIECES[piece])
        if step == 1:
            src = source(sl, blocks)
        else:
            src = y_bufs[sl][2 * step - (4 if up else 3)].at[blocks]
        dst = y_bufs[sl][6 if step == 4 else 2 * step - (2 if up else 1)].at[blocks]
        n = (step - 1) * 4 + (0 if up else 2) + piece
        return remote(src, dst, y_s.at[sl, n], y_r.at[sl, n], y_up if up else y_down)

    def moves(step):
        return [(piece, up) for piece in (0, 1) for up in (True, False) if step < 4 or (step == 4 and up == (piece == 0))]

    def y_begin(sl):
        for piece, up in moves(1):
            start(y_copy(sl, 1, up, piece))

    def y_step(sl, step):
        for piece, up in moves(step):
            y_copy(sl, step, up, piece).wait_recv()
            if (piece, up) in moves(step + 1):
                start(y_copy(sl, step + 1, up, piece))

    def x_step(sl, step):
        ks = STEP_KS[step]
        first, size = 2 * ks[0], 2 * len(ks)

        def fill(j, _):
            for k in ks:
                for slot in range(2):
                    stage[sl][(j - 1) * SLOTS + 2 * k + slot] = load(sl, k, send_t[j, 2 * k + slot])
            return 0

        lax.fori_loop(1, COLS, fill, 0)
        for j in order:
            remote(
                stage[sl].at[pl.ds((j - 1) * SLOTS + first, size)],
                land[sl].at[pl.ds(j * SLOTS + first, size)],
                x_s.at[sl],
                x_r.at[sl],
                row[j],
            ).start()
        for k in ks:
            for slot in range(2):
                land[sl][2 * k + slot] = load(sl, k, send_t[0, 2 * k + slot])

    def x_whole(sl):
        return remote(
            stage[sl].at[...], land[sl].at[pl.ds(SLOTS, (COLS - 1) * SLOTS)], x_s.at[sl], x_r.at[sl], row[1]
        )

    glob_at = []
    for g in range(G):
        block = glob[g]
        group = block // PER
        dy_g = (group // NC) % NY + NY - y
        dy_g = jnp.where(dy_g >= NY, dy_g - NY, dy_g)
        k_g = jnp.where(dy_g < 4, 2 * dy_g, jnp.where(dy_g == 4, 7, 15 - 2 * dy_g))
        dx_g = group // (NY * NC) + NX - x
        dx_g = jnp.where(dx_g >= NX, dx_g - NX, dx_g)
        glob_at.append((k_g, block % PER, dx_g, group % NC))

    def g_begin(sl):
        for g, (k_g, off, _, _) in enumerate(glob_at):
            block = load(sl, 0, off)
            for k in range(1, NY):
                block = jnp.where(k_g == k, load(sl, k, off), block)
            g_out[sl][g] = block
        for dx in (2, 1, 3):
            remote(g_out[sl], g_in[sl].at[pl.ds((dx - 1) * G, G)], g_s.at[sl], g_r.at[sl], row[dx * NC]).start()

    def g_whole(sl):
        return remote(g_in[sl], g_in[sl], g_s.at[sl], g_r.at[sl], row[NC])

    def g_cores(sl):
        return remote(g_sel[sl], g_other[sl], c_s.at[sl], c_r.at[sl], row[1])

    def g_mid(sl):
        g_whole(sl).wait_recv()
        for g, (_, _, dx_g, _) in enumerate(glob_at):
            block = g_out[sl][g]
            for dx in (1, 2, 3):
                block = jnp.where(dx_g == dx, g_in[sl][(dx - 1) * G + g], block)
            g_sel[sl][g] = block
        g_cores(sl).start()

    def g_end(sl):
        g_cores(sl).wait_recv()
        for g, (_, _, _, c_g) in enumerate(glob_at):
            g_fin[sl][g] = jnp.where(c_g == c, g_sel[sl][g], g_other[sl][g])

    halo = [[] for _ in range(5)]

    def edges(sl):
        for n, (src, dst, to) in enumerate(((PER - 1, 0, ahead), (0, PER + 1, behind))):
            copy = remote(source(sl, src), pads[sl].at[dst], h_s.at[sl, n], h_r.at[sl, n], to)
            copy.start()
            halo[sl].append(copy)

        def fill(i, _):
            pads[sl][i + 1] = load(sl, 0, i)
            return 0

        lax.fori_loop(0, PER, fill, 0)

    def ready(sl):
        for copy in halo[sl]:
            copy.wait_recv()
        x_whole(sl).wait_recv()
        g_end(sl)

    def pack():
        low = lax.broadcasted_iota(jnp.int32, (HALF, DH), 1) < BLOCK

        def one(i, _):
            top = v_ref[i, pl.ds(0, HALF), pl.ds(DH, DH)].astype(jnp.float32)
            bottom = v_ref[i, pl.ds(HALF, HALF), pl.ds(DH, DH)].astype(jnp.float32)
            packed[0][i] = jnp.where(low, top, pltpu.roll(bottom, BLOCK, 1)).astype(BF16)
            packed[1][i] = jnp.where(low, pltpu.roll(top, BLOCK, 1), bottom).astype(BF16)
            return 0

        lax.fori_loop(0, PER, one, 0)

    def gathered(sl, i):
        return (
            [pads[sl][i], pads[sl][i + 1], pads[sl][i + 2]]
            + [g_fin[sl][g] for g in range(G)]
            + [land[sl][read_t[0, n * 32 + i]] for n in range(R)]
        )

    def scores(h, begin, end):
        def one(i, _):
            blocks = gathered(K1 if h else K0, i)
            if h:
                blocks = [b[:HALF] for b in blocks] + [b[HALF:] for b in blocks]
            s = lax.dot_general(
                q_ref[i, :, pl.ds(h * DH, DH)],
                jnp.concatenate(blocks, axis=0),
                (((1,), (1,)), ((), ())),
                preferred_element_type=jnp.float32,
            )
            s = s * SCALE
            e = jnp.exp(s - jnp.max(s, axis=1, keepdims=True))
            t_bufs[h][i] = jnp.broadcast_to(jnp.sum(e, axis=1, keepdims=True), (BLOCK, DH))
            p_bufs[h][i] = e.astype(BF16)
            return 0

        lax.fori_loop(begin, end, one, 0)

    def context0(begin, end):
        def one(i, _):
            o = jnp.dot(p_bufs[0][i], jnp.concatenate(gathered(V0, i), axis=0), preferred_element_type=jnp.float32)
            rows = pl.ds(pl.multiple_of(i * BLOCK, BLOCK), BLOCK)
            ctx[0][rows, pl.ds(0, DH)] = (o / t_bufs[0][i]).astype(BF16)
            return 0

        lax.fori_loop(begin, end, one, 0)

    def context1(a, begin, end):
        low = lax.broadcasted_iota(jnp.int32, (HALF, DH), 1) < BLOCK
        half_keys = KEYS // 2

        def one(i, _):
            p = jnp.concatenate([p_bufs[1][i, :, pl.ds(0, half_keys)], p_bufs[1][i, :, pl.ds(half_keys, half_keys)]])
            o = jnp.dot(p, jnp.concatenate(gathered(V1A + a, i), axis=0), preferred_element_type=jnp.float32)
            upper = o[0:HALF] + pltpu.roll(o[BLOCK : BLOCK + HALF], BLOCK, 1)
            lower = pltpu.roll(o[HALF:BLOCK], BLOCK, 1) + o[BLOCK + HALF :]
            total = jnp.where(low, t_bufs[1][i, pl.ds(0, HALF)], t_bufs[1][i, pl.ds(HALF, HALF)])
            rows = pl.ds(pl.multiple_of(i * HALF, HALF), HALF)
            ctx[1 + a][rows, pl.ds(0, DH)] = (jnp.where(low, upper, lower) / total).astype(BF16)
            return 0

        lax.fori_loop(begin, end, one, 0)

    def z_copy(t, step, up, piece):
        height = HALF if t else BLOCK
        first, size = PIECES[piece]
        rows = pl.ds(first * height, size * height)
        from_k = 0 if step == 1 else 2 * step - (3 if up else 2)
        to_k = 7 if step == 4 else 2 * step - (1 if up else 0)
        n = (step - 1) * 4 + (0 if up else 2) + piece
        return remote(
            ctx[t].at[rows, pl.ds(from_k * DH, DH)],
            ctx[t].at[rows, pl.ds(to_k * DH, DH)],
            z_s.at[t, n],
            z_r.at[t, n],
            z_up if up else z_down,
        )

    def z_begin(t, piece):
        for up in (True, False):
            start(z_copy(t, 1, up, piece))

    def z_step(t, step, only=None):
        for piece, up in moves(step):
            if only is not None and piece != only:
                continue
            z_copy(t, step, up, piece).wait_recv()
            if (piece, up) in moves(step + 1):
                start(z_copy(t, step + 1, up, piece))

    def project0():
        def tile(n, _):
            rows = pl.ds(pl.multiple_of(n * TILE, 16), TILE)
            acc[rows, :] = jnp.dot(ctx[0][rows, :], w_lo[0][...], preferred_element_type=jnp.float32)
            return 0

        lax.fori_loop(0, ROWS // TILE, tile, 0)

    def project1(a, k0, k1, last=False):
        cols = pl.ds(k0 * DH, (k1 - k0) * DH)
        for b0, b1 in ((0, 6), (6, 12), (12, PER)):
            lhs = ctx[1 + a][pl.ds(b0 * HALF, (b1 - b0) * HALF), cols]
            for w, shift in ((w_lo[1 + a], 0), (w_hi[a], HALF)):
                part = jnp.dot(lhs, w[cols, :], preferred_element_type=jnp.float32)
                for b in range(b0, b1):
                    rows = pl.ds(b * BLOCK + shift, HALF)
                    total = acc[rows, :] + part[(b - b0) * HALF : (b - b0 + 1) * HALF]
                    if last:
                        out_ref[rows, :] = total.astype(out_ref.dtype)
                    else:
                        acc[rows, :] = total

    def tables():
        lane = lax.broadcasted_iota(jnp.int32, (COLS, DH), 1)

        def requests(holders):
            rs = [jnp.concatenate([code_ref[r, pl.ds(at, 1), :] for at in holders], axis=0) for r in range(R)]
            return jnp.where(lane < 32, rs[0], jnp.where(lane < 64, pltpu.roll(rs[1], 32, 1), pltpu.roll(rs[2], 64, 1)))

        asked = requests([row[j][0] for j in range(COLS)])
        ranked = lane * 32 + (asked & 31)
        asked = asked >> 5
        table = jnp.zeros((COLS, DH), jnp.int32)
        for k in range(NY):
            match = asked == dev(dy=Y_OF_K[k] + NY)[0]
            first = jnp.min(jnp.where(match, ranked, 1 << 12), axis=1, keepdims=True) & 31
            last = jnp.max(jnp.where(match, ranked, 0), axis=1, keepdims=True) & 31
            table = jnp.where(lane == 2 * k, first, jnp.where(lane == 2 * k + 1, last, table))
        send_v[...] = table
        mine = requests([seq] * COLS) >> 5
        rank = jnp.zeros((COLS, DH), jnp.int32)
        for d in range(1, 32 * (R - 1) + PER):
            rank = rank + jnp.where((pltpu.roll(mine, d, 1) == mine) & (lane >= d), 1, 0)
        column = (((mine >> 4) - x) & 3) * NC + (((mine & 1) - c) & 1)
        dy = (((mine >> 1) & 7) - y) & 7
        ring = jnp.where(dy < 4, 2 * dy, jnp.where(dy == 4, 7, 15 - 2 * dy))
        read_v[...] = column * SLOTS + 2 * ring + jnp.minimum(rank, 1)
        t_copies = [
            pltpu.make_async_copy(send_v, send_t, i_s.at[3]),
            pltpu.make_async_copy(read_v, read_t, i_s.at[4]),
        ]
        for copy in t_copies:
            copy.start()
        for copy in t_copies:
            copy.wait()

    y_begin(K0)
    tables()
    x_step(K0, 0)
    edges(K0)
    in_copies[1].wait()
    in_copies[2].wait()
    x_step(V0, 0)
    edges(V0)
    x_step(K1, 0)
    edges(K1)
    y_step(K0, 1)
    y_begin(V0)
    x_step(K0, 1)
    pack()
    w_begin()
    edges(V1A)
    edges(V1B)
    y_step(K0, 2)
    x_step(K0, 2)
    y_step(V0, 1)
    x_step(V0, 1)
    x_step(V1A, 0)
    x_step(V1B, 0)
    y_step(K0, 3)
    x_step(K0, 3)
    y_step(V0, 2)
    x_step(V0, 2)
    w_zeros()
    y_step(K0, 4)
    g_begin(K0)
    x_step(K0, 4)
    y_step(V0, 3)
    y_begin(K1)
    x_step(V0, 3)
    g_mid(K0)
    y_step(V0, 4)
    y_begin(V1A)
    g_begin(V0)
    x_step(V0, 4)
    ready(K0)
    scores(0, 0, 6)
    y_step(K1, 1)
    x_step(K1, 1)
    scores(0, 6, 12)
    g_mid(V0)
    y_step(K1, 2)
    x_step(K1, 2)
    scores(0, 12, 17)
    y_step(V1A, 1)
    x_step(V1A, 1)
    ready(V0)
    context0(0, CUT)
    z_begin(0, 0)
    context0(CUT, PER)
    z_begin(0, 1)
    y_step(K1, 3)
    x_step(K1, 3)
    z_step(0, 1, 0)
    y_step(V1A, 2)
    x_step(V1A, 2)
    z_step(0, 1, 1)
    y_step(K1, 4)
    y_begin(V1B)
    g_begin(K1)
    x_step(K1, 4)
    z_step(0, 2, 0)
    y_step(V1A, 3)
    x_step(V1A, 3)
    z_step(0, 2, 1)
    g_mid(K1)
    y_step(V1A, 4)
    g_begin(V1A)
    x_step(V1A, 4)
    y_step(V1B, 1)
    x_step(V1B, 1)
    z_step(0, 3, 0)
    ready(K1)
    scores(1, 0, 4)
    z_step(0, 3, 1)
    y_step(V1B, 2)
    x_step(V1B, 2)
    g_mid(V1A)
    scores(1, 4, 8)
    y_step(V1B, 3)
    x_step(V1B, 3)
    z_step(0, 4)
    scores(1, 8, 12)
    y_step(V1B, 4)
    g_begin(V1B)
    x_step(V1B, 4)
    scores(1, 12, 17)
    ready(V1A)
    context1(0, 0, CUT)
    z_begin(1, 0)
    context1(0, CUT, PER)
    z_begin(1, 1)
    g_mid(V1B)
    for copy in w_copies:
        copy.wait()
    z_step(1, 1)
    ready(V1B)
    context1(1, 0, CUT)
    z_begin(2, 0)
    z_step(1, 2)
    context1(1, CUT, PER)
    z_begin(2, 1)
    z_step(1, 3)
    project0()
    z_step(1, 4)
    z_step(2, 1)
    project1(0, 0, 8)
    z_step(2, 2)
    project1(1, 0, 5)
    z_step(2, 3)
    project1(1, 5, 7)
    z_step(2, 4)
    project1(1, 7, 8, last=True)

    for copy in pending:
        copy.wait_send()
    for sl in range(5):
        for copy in halo[sl]:
            copy.wait_send()
        x_whole(sl).wait_send()
        g_whole(sl).wait_send()
        g_cores(sl).wait_send()


def on_device(queries, keys, values, rand_group, rand_offset, glob_blocks, w_out):
    n_seq = NX * NY * NC
    code = (rand_group * 32 + rand_offset).T.reshape(R, n_seq, PER)
    code = jnp.pad(code, ((0, 0), (0, 0), (0, DH - PER)), constant_values=-1)
    shape = (PER, BLOCK, HEADS * DH)
    features = w_out.shape[1]
    vmem = pltpu.VMEM

    def per_slice(blocks):
        return [vmem((blocks, height, DH), BF16) for height in HEIGHT]

    scratch = [vmem(shape, BF16)] * 3 + [vmem((COLS, DH), jnp.int32)] * 2 + [pltpu.SMEM((COLS, DH), jnp.int32)] * 2
    scratch += [vmem((PER, height, DH), BF16) for height in HEIGHT for _ in range(NY - 1)]
    for blocks in ((COLS - 1) * SLOTS, COLS * SLOTS, PER + 2, G, 3 * G, G, G, G):
        scratch += per_slice(blocks)
    scratch += [vmem((PER, HALF, DH), BF16)] * 2
    scratch += [vmem((PER, BLOCK, KEYS), BF16)] * 2
    scratch += [vmem((PER, BLOCK, DH), jnp.float32)] * 2
    scratch += [vmem((ROWS, NZ * DH), BF16)] + [vmem((PER * HALF, NZ * DH), BF16)] * 2
    scratch += [vmem((NZ * DH, features), BF16)] * 5
    scratch += [vmem((ROWS, features), jnp.float32)]
    dma = pltpu.SemaphoreType.DMA
    scratch += [dma((5, 16)), dma((5, 16))] + [dma((5,))] * 6 + [dma((5, 2))] * 2
    scratch += [dma((3, 16)), dma((3, 16)), dma((5 * NZ,)), dma((5,))]
    hbm = pl.BlockSpec(memory_space=pl.ANY)
    whole = pl.BlockSpec(memory_space=vmem)
    return pl.pallas_call(
        kernel,
        out_shape=jax.ShapeDtypeStruct((ROWS, features), BF16),
        in_specs=[pl.BlockSpec(memory_space=pltpu.SMEM), whole, hbm, hbm, hbm, hbm],
        out_specs=whole,
        scratch_shapes=scratch,
        compiler_params=pltpu.CompilerParams(collective_id=0, has_side_effects=True, vmem_limit_bytes=60 << 20),
        name="sparse_attention",
    )(glob_blocks, code, queries.reshape(shape), keys.reshape(shape), values.reshape(shape), w_out)


def solution(mesh):
    return jax.shard_map(
        on_device,
        mesh=mesh,
        in_specs=(P("seq", "head"), P("seq", "head"), P("seq", "head"), P(), P(), P(), P(None, "head")),
        out_specs=P("seq", "head"),
        check_vma=False,
    )
```

```python
import math

import jax
import jax.numpy as jnp
from jax import lax
from jax.experimental import pallas as pl
from jax.experimental.pallas import tpu as pltpu
from jax.sharding import PartitionSpec as P

MESH = pl.DeviceIdType.MESH
DH = 128
BLOCK = 64
R = 3
G = 2
NX, NY, NC, NZ = 4, 8, 2, 8
PER = 17
ROWS = PER * BLOCK
HEADS = 2
COLS = NX * NC
SLOTS = 2 * NY
KEYS = 8 * BLOCK
CUT = 9
PIECES = ((0, CUT), (CUT, PER - CUT))
SCALE = 1.0 / math.sqrt(DH)
STEP_KS = ((0,), (1, 2), (3, 4), (5, 6), (7,))
Y_OF_K = (0, -1, 1, -2, 2, -3, 3, 4)
K0, V0, K1, V1 = range(4)
TILE = 272
BF16 = jnp.bfloat16


def place():
    seq = lax.axis_index("seq")
    return seq // (NY * NC), (seq // NC) % NY, seq % NC, lax.axis_index("head")


def kernel(*refs):
    glob, code_ref, q_hbm, k_hbm, v_hbm, w_ref, out_ref, *refs = refs
    q_ref, k_ref, v_ref, send_v, read_v, send_t, read_t, *refs = refs
    y_bufs = [refs[7 * sl : 7 * sl + 7] for sl in range(4)]
    refs = refs[28:]
    stage, land, pads, g_out, g_in, g_sel, g_other, g_fin = [refs[4 * n : 4 * n + 4] for n in range(8)]
    refs = refs[32:]
    p_bufs, t_bufs, ctx, w_bufs, refs = refs[0:2], refs[2:4], refs[4:6], refs[6:8], refs[8:]
    acc, y_s, y_r, x_s, x_r, g_s, g_r, c_s, c_r, h_s, h_r, z_s, z_r, w_s, i_s = refs
    x, y, c, z = place()
    seq = lax.axis_index("seq")

    def dev(dx=0, dy=0, dc=0, dz=0):
        return (((x + dx) % NX * NY + (y + dy) % NY) * NC + (c + dc) % NC, (z + dz) % NZ)

    n_seq = NX * NY * NC
    ahead, behind = ((seq + 1) % n_seq, z), ((seq + n_seq - 1) % n_seq, z)
    y_up, y_down, z_up, z_down = dev(dy=1), dev(dy=NY - 1), dev(dz=1), dev(dz=NZ - 1)
    row = [dev(dx=NX - j // NC, dc=NC - j % NC) for j in range(COLS)]
    order = (4, 5, 2, 3, 6, 7, 1)

    def remote(src, dst, s, r, to):
        return pltpu.make_async_remote_copy(
            src_ref=src, dst_ref=dst, send_sem=s, recv_sem=r, device_id=to, device_id_type=MESH
        )

    peers = [y_up, y_down, z_up, z_down, ahead, behind] + row[1:]
    barrier = pltpu.get_barrier_semaphore()
    for peer in peers:
        pl.semaphore_signal(barrier, inc=1, device_id=peer, device_id_type=MESH)

    in_copies = [
        pltpu.make_async_copy(src, dst, i_s.at[n])
        for n, (src, dst) in enumerate(((k_hbm, k_ref), (v_hbm, v_ref), (q_hbm, q_ref)))
    ]
    for copy in in_copies:
        copy.start()

    w_copies = []

    def w_begin():
        for h in range(HEADS):
            for k in range(NZ):
                at = ((z + Y_OF_K[k] + NZ) % NZ * HEADS + h) * DH
                src = w_ref.at[pl.ds(pl.multiple_of(at, DH), DH)]
                copy = pltpu.make_async_copy(src, w_bufs[h].at[pl.ds(k * DH, DH)], w_s.at[len(w_copies)])
                copy.start()
                w_copies.append(copy)

    in_copies[0].wait()
    pl.semaphore_wait(barrier, len(peers))

    def columns(sl):
        return pl.ds(DH if sl in (K1, V1) else 0, DH)

    def source(sl, blocks):
        return (k_ref if sl in (K0, K1) else v_ref).at[blocks, :, columns(sl)]

    def load(sl, k, off):
        if k:
            return y_bufs[sl][k - 1][off]
        return (k_ref if sl in (K0, K1) else v_ref)[off, :, columns(sl)]

    pending = []

    def start(copy):
        copy.start()
        pending.append(copy)

    def y_copy(sl, step, up, piece):
        blocks = pl.ds(*PIECES[piece])
        if step == 1:
            src = source(sl, blocks)
        else:
            src = y_bufs[sl][2 * step - (4 if up else 3)].at[blocks]
        dst = y_bufs[sl][6 if step == 4 else 2 * step - (2 if up else 1)].at[blocks]
        n = (step - 1) * 4 + (0 if up else 2) + piece
        return remote(src, dst, y_s.at[sl, n], y_r.at[sl, n], y_up if up else y_down)

    def moves(step):
        return [(piece, up) for piece in (0, 1) for up in (True, False) if step < 4 or (step == 4 and up == (piece == 0))]

    def y_begin(sl):
        for piece, up in moves(1):
            start(y_copy(sl, 1, up, piece))

    def y_step(sl, step):
        for piece, up in moves(step):
            y_copy(sl, step, up, piece).wait_recv()
            if (piece, up) in moves(step + 1):
                start(y_copy(sl, step + 1, up, piece))

    def x_step(sl, step):
        ks = STEP_KS[step]
        first, size = 2 * ks[0], 2 * len(ks)

        def fill(j, _):
            for k in ks:
                for slot in range(2):
                    stage[sl][(j - 1) * SLOTS + 2 * k + slot] = load(sl, k, send_t[j, 2 * k + slot])
            return 0

        lax.fori_loop(1, COLS, fill, 0)
        for j in order:
            remote(
                stage[sl].at[pl.ds((j - 1) * SLOTS + first, size)],
                land[sl].at[pl.ds(j * SLOTS + first, size)],
                x_s.at[sl],
                x_r.at[sl],
                row[j],
            ).start()
        for k in ks:
            for slot in range(2):
                land[sl][2 * k + slot] = load(sl, k, send_t[0, 2 * k + slot])

    def x_whole(sl):
        return remote(
            stage[sl].at[...], land[sl].at[pl.ds(SLOTS, (COLS - 1) * SLOTS)], x_s.at[sl], x_r.at[sl], row[1]
        )

    glob_at = []
    for g in range(G):
        block = glob[g]
        group = block // PER
        dy_g = (group // NC) % NY + NY - y
        dy_g = jnp.where(dy_g >= NY, dy_g - NY, dy_g)
        k_g = jnp.where(dy_g < 4, 2 * dy_g, jnp.where(dy_g == 4, 7, 15 - 2 * dy_g))
        dx_g = group // (NY * NC) + NX - x
        dx_g = jnp.where(dx_g >= NX, dx_g - NX, dx_g)
        glob_at.append((k_g, block % PER, dx_g, group % NC))

    def g_begin(sl):
        for g, (k_g, off, _, _) in enumerate(glob_at):
            block = load(sl, 0, off)
            for k in range(1, NY):
                block = jnp.where(k_g == k, load(sl, k, off), block)
            g_out[sl][g] = block
        for dx in (2, 1, 3):
            remote(g_out[sl], g_in[sl].at[pl.ds((dx - 1) * G, G)], g_s.at[sl], g_r.at[sl], row[dx * NC]).start()

    def g_whole(sl):
        return remote(g_in[sl], g_in[sl], g_s.at[sl], g_r.at[sl], row[NC])

    def g_cores(sl):
        return remote(g_sel[sl], g_other[sl], c_s.at[sl], c_r.at[sl], row[1])

    def g_mid(sl):
        g_whole(sl).wait_recv()
        for g, (_, _, dx_g, _) in enumerate(glob_at):
            block = g_out[sl][g]
            for dx in (1, 2, 3):
                block = jnp.where(dx_g == dx, g_in[sl][(dx - 1) * G + g], block)
            g_sel[sl][g] = block
        g_cores(sl).start()

    def g_end(sl):
        g_cores(sl).wait_recv()
        for g, (_, _, _, c_g) in enumerate(glob_at):
            g_fin[sl][g] = jnp.where(c_g == c, g_sel[sl][g], g_other[sl][g])

    halo = [[] for _ in range(4)]

    def edges(sl):
        for n, (src, dst, to) in enumerate(((PER - 1, 0, ahead), (0, PER + 1, behind))):
            copy = remote(source(sl, src), pads[sl].at[dst], h_s.at[sl, n], h_r.at[sl, n], to)
            copy.start()
            halo[sl].append(copy)

        def fill(i, _):
            pads[sl][i + 1] = load(sl, 0, i)
            return 0

        lax.fori_loop(0, PER, fill, 0)

    def ready(sl):
        for copy in halo[sl]:
            copy.wait_recv()
        x_whole(sl).wait_recv()
        g_end(sl)

    def gathered(sl, i):
        return (
            [pads[sl][i], pads[sl][i + 1], pads[sl][i + 2]]
            + [g_fin[sl][g] for g in range(G)]
            + [land[sl][read_t[0, n * 32 + i]] for n in range(R)]
        )

    def scores(h, begin, end):
        def one(i, _):
            blocks = gathered(K1 if h else K0, i)
            s = lax.dot_general(
                q_ref[i, :, pl.ds(h * DH, DH)],
                jnp.concatenate(blocks, axis=0),
                (((1,), (1,)), ((), ())),
                preferred_element_type=jnp.float32,
            )
            s = s * SCALE
            e = jnp.exp(s - jnp.max(s, axis=1, keepdims=True))
            t_bufs[h][i] = jnp.broadcast_to(jnp.sum(e, axis=1, keepdims=True), (BLOCK, DH))
            p_bufs[h][i] = e.astype(BF16)
            return 0

        lax.fori_loop(begin, end, one, 0)

    def context(h, begin, end):
        def one(i, _):
            blocks = gathered(V1 if h else V0, i)
            o = jnp.dot(p_bufs[h][i], jnp.concatenate(blocks, axis=0), preferred_element_type=jnp.float32)
            rows = pl.ds(pl.multiple_of(i * BLOCK, BLOCK), BLOCK)
            ctx[h][rows, pl.ds(0, DH)] = (o / t_bufs[h][i]).astype(BF16)
            return 0

        lax.fori_loop(begin, end, one, 0)

    def z_copy(t, step, up, piece):
        first, size = PIECES[piece]
        rows = pl.ds(first * BLOCK, size * BLOCK)
        from_k = 0 if step == 1 else 2 * step - (3 if up else 2)
        to_k = 7 if step == 4 else 2 * step - (1 if up else 0)
        n = (step - 1) * 4 + (0 if up else 2) + piece
        return remote(
            ctx[t].at[rows, pl.ds(from_k * DH, DH)],
            ctx[t].at[rows, pl.ds(to_k * DH, DH)],
            z_s.at[t, n],
            z_r.at[t, n],
            z_up if up else z_down,
        )

    def z_begin(t, piece):
        for up in (True, False):
            start(z_copy(t, 1, up, piece))

    def z_step(t, step, only=None):
        for piece, up in moves(step):
            if only is not None and piece != only:
                continue
            z_copy(t, step, up, piece).wait_recv()
            if (piece, up) in moves(step + 1):
                start(z_copy(t, step + 1, up, piece))

    def project(h, k0, k1, begin=0, end=ROWS // TILE, first=False, last=False):
        cols = pl.ds(k0 * DH, (k1 - k0) * DH)

        def tile(n, _):
            rows = pl.ds(pl.multiple_of(n * TILE, 16), TILE)
            part = jnp.dot(ctx[h][rows, cols], w_bufs[h][cols, :], preferred_element_type=jnp.float32)
            if not first:
                part = part + acc[rows, :]
            if last:
                out_ref[rows, :] = part.astype(out_ref.dtype)
            else:
                acc[rows, :] = part
            return 0

        lax.fori_loop(begin, end, tile, 0)

    def tables():
        lane = lax.broadcasted_iota(jnp.int32, (COLS, DH), 1)

        def requests(holders):
            rs = [jnp.concatenate([code_ref[r, pl.ds(at, 1), :] for at in holders], axis=0) for r in range(R)]
            return jnp.where(lane < 32, rs[0], jnp.where(lane < 64, pltpu.roll(rs[1], 32, 1), pltpu.roll(rs[2], 64, 1)))

        asked = requests([row[j][0] for j in range(COLS)])
        ranked = lane * 32 + (asked & 31)
        asked = asked >> 5
        table = jnp.zeros((COLS, DH), jnp.int32)
        for k in range(NY):
            match = asked == dev(dy=Y_OF_K[k] + NY)[0]
            first = jnp.min(jnp.where(match, ranked, 1 << 12), axis=1, keepdims=True) & 31
            last = jnp.max(jnp.where(match, ranked, 0), axis=1, keepdims=True) & 31
            table = jnp.where(lane == 2 * k, first, jnp.where(lane == 2 * k + 1, last, table))
        send_v[...] = table
        mine = requests([seq] * COLS) >> 5
        rank = jnp.zeros((COLS, DH), jnp.int32)
        for d in range(1, 32 * (R - 1) + PER):
            rank = rank + jnp.where((pltpu.roll(mine, d, 1) == mine) & (lane >= d), 1, 0)
        column = (((mine >> 4) - x) & 3) * NC + (((mine & 1) - c) & 1)
        dy = (((mine >> 1) & 7) - y) & 7
        ring = jnp.where(dy < 4, 2 * dy, jnp.where(dy == 4, 7, 15 - 2 * dy))
        read_v[...] = column * SLOTS + 2 * ring + jnp.minimum(rank, 1)
        t_copies = [
            pltpu.make_async_copy(send_v, send_t, i_s.at[3]),
            pltpu.make_async_copy(read_v, read_t, i_s.at[4]),
        ]
        for copy in t_copies:
            copy.start()
        for copy in t_copies:
            copy.wait()

    y_begin(K0)
    tables()
    x_step(K0, 0)
    edges(K0)
    in_copies[1].wait()
    in_copies[2].wait()
    x_step(V0, 0)
    edges(V0)
    x_step(K1, 0)
    edges(K1)
    y_step(K0, 1)
    x_step(K0, 1)
    w_begin()
    edges(V1)
    y_step(K0, 2)
    y_begin(V0)
    x_step(K0, 2)
    x_step(V1, 0)
    y_step(K0, 3)
    x_step(K0, 3)
    y_step(V0, 1)
    x_step(V0, 1)
    y_step(K0, 4)
    g_begin(K0)
    x_step(K0, 4)
    y_step(V0, 2)
    y_begin(K1)
    x_step(V0, 2)
    g_mid(K0)
    y_step(V0, 3)
    x_step(V0, 3)
    ready(K0)
    scores(0, 0, 5)
    y_step(K1, 1)
    x_step(K1, 1)
    scores(0, 5, 9)
    y_step(V0, 4)
    g_begin(V0)
    x_step(V0, 4)
    scores(0, 9, 13)
    y_step(K1, 2)
    y_begin(V1)
    x_step(K1, 2)
    scores(0, 13, 17)
    g_mid(V0)
    y_step(K1, 3)
    x_step(K1, 3)
    ready(V0)
    context(0, 0, CUT)
    z_begin(0, 0)
    context(0, CUT, PER)
    z_begin(0, 1)
    y_step(V1, 1)
    x_step(V1, 1)
    y_step(K1, 4)
    g_begin(K1)
    x_step(K1, 4)
    z_step(0, 1)
    y_step(V1, 2)
    x_step(V1, 2)
    g_mid(K1)
    z_step(0, 2)
    y_step(V1, 3)
    x_step(V1, 3)
    ready(K1)
    scores(1, 0, 5)
    z_step(0, 3)
    y_step(V1, 4)
    g_begin(V1)
    x_step(V1, 4)
    scores(1, 5, 11)
    g_mid(V1)
    scores(1, 11, 17)
    z_step(0, 4)
    for copy in w_copies:
        copy.wait()
    ready(V1)
    context(1, 0, CUT)
    z_begin(1, 0)
    context(1, CUT, PER)
    z_begin(1, 1)
    project(0, 0, 8, 0, 2, first=True)
    z_step(1, 1, 0)
    z_step(1, 1, 1)
    project(0, 0, 8, 2, 4, first=True)
    z_step(1, 2)
    project(1, 0, 5)
    z_step(1, 3)
    project(1, 5, 7)
    z_step(1, 4)
    project(1, 7, 8, last=True)

    for copy in pending:
        copy.wait_send()
    for sl in range(4):
        for copy in halo[sl]:
            copy.wait_send()
        x_whole(sl).wait_send()
        g_whole(sl).wait_send()
        g_cores(sl).wait_send()


def on_device(queries, keys, values, rand_group, rand_offset, glob_blocks, w_out):
    n_seq = NX * NY * NC
    code = (rand_group * 32 + rand_offset).T.reshape(R, n_seq, PER)
    code = jnp.pad(code, ((0, 0), (0, 0), (0, DH - PER)), constant_values=-1)
    shape = (PER, BLOCK, HEADS * DH)
    features = w_out.shape[1]
    vmem = pltpu.VMEM

    def per_slice(blocks):
        return [vmem((blocks, BLOCK, DH), BF16)] * 4

    scratch = [vmem(shape, BF16)] * 3 + [vmem((COLS, DH), jnp.int32)] * 2 + [pltpu.SMEM((COLS, DH), jnp.int32)] * 2
    scratch += per_slice(PER) * (NY - 1)
    for blocks in ((COLS - 1) * SLOTS, COLS * SLOTS, PER + 2, G, 3 * G, G, G, G):
        scratch += per_slice(blocks)
    scratch += [vmem((PER, BLOCK, KEYS), BF16)] * 2
    scratch += [vmem((PER, BLOCK, DH), jnp.float32)] * 2
    scratch += [vmem((ROWS, NZ * DH), BF16)] * 2
    scratch += [vmem((NZ * DH, features), BF16)] * 2
    scratch += [vmem((ROWS, features), jnp.float32)]
    dma = pltpu.SemaphoreType.DMA
    scratch += [dma((4, 16)), dma((4, 16))] + [dma((4,))] * 6 + [dma((4, 2))] * 2
    scratch += [dma((2, 16)), dma((2, 16)), dma((HEADS * NZ,)), dma((5,))]
    hbm = pl.BlockSpec(memory_space=pl.ANY)
    whole = pl.BlockSpec(memory_space=vmem)
    return pl.pallas_call(
        kernel,
        out_shape=jax.ShapeDtypeStruct((ROWS, features), BF16),
        in_specs=[pl.BlockSpec(memory_space=pltpu.SMEM), whole, hbm, hbm, hbm, hbm],
        out_specs=whole,
        scratch_shapes=scratch,
        compiler_params=pltpu.CompilerParams(collective_id=0, has_side_effects=True, vmem_limit_bytes=60 << 20),
        name="sparse_attention",
    )(glob_blocks, code, queries.reshape(shape), keys.reshape(shape), values.reshape(shape), w_out)


def solution(mesh):
    return jax.shard_map(
        on_device,
        mesh=mesh,
        in_specs=(P("seq", "head"), P("seq", "head"), P("seq", "head"), P(), P(), P(), P(None, "head")),
        out_specs=P("seq", "head"),
        check_vma=False,
    )
```

```python
import math

import jax
import jax.numpy as jnp
from jax import lax
from jax.experimental import pallas as pl
from jax.experimental.pallas import tpu as pltpu
from jax.sharding import PartitionSpec as P

MESH = pl.DeviceIdType.MESH
DH = 128
BLOCK = 64
R = 3
G = 2
NX, NY, NC, NZ = 4, 8, 2, 8
PER = 17
ROWS = PER * BLOCK
HEADS = 2
COLS = NX * NC
SLOTS = 2 * NY
KEYS = 8 * BLOCK
CUT = 9
PIECES = ((0, CUT), (CUT, PER - CUT))
LAST_PIECES = ((0, 5), (5, 4), (9, 4), (13, 4))
SCALE = 1.0 / math.sqrt(DH)
STEP_KS = ((0,), (1, 2), (3, 4), (5, 6), (7,))
Y_OF_K = (0, -1, 1, -2, 2, -3, 3, 4)
K0, V0, K1, V1 = range(4)
TILE = 272
BF16 = jnp.bfloat16


def place():
    seq = lax.axis_index("seq")
    return seq // (NY * NC), (seq // NC) % NY, seq % NC, lax.axis_index("head")


def kernel(*refs):
    glob, code_ref, q_hbm, k_hbm, v_hbm, w_ref, out_ref, *refs = refs
    q_ref, k_ref, v_ref, send_v, read_v, send_t, read_t, *refs = refs
    y_bufs = [refs[7 * sl : 7 * sl + 7] for sl in range(4)]
    refs = refs[28:]
    stage, land, pads, g_out, g_in, g_sel, g_other, g_fin = [refs[4 * n : 4 * n + 4] for n in range(8)]
    refs = refs[32:]
    p_bufs, t_bufs, ctx, w_bufs, refs = refs[0:2], refs[2:4], refs[4:6], refs[6:8], refs[8:]
    acc, y_s, y_r, x_s, x_r, g_s, g_r, c_s, c_r, h_s, h_r, z_s, z_r, w_s, i_s = refs
    x, y, c, z = place()
    seq = lax.axis_index("seq")

    def dev(dx=0, dy=0, dc=0, dz=0):
        return (((x + dx) % NX * NY + (y + dy) % NY) * NC + (c + dc) % NC, (z + dz) % NZ)

    n_seq = NX * NY * NC
    ahead, behind = ((seq + 1) % n_seq, z), ((seq + n_seq - 1) % n_seq, z)
    y_up, y_down, z_up, z_down = dev(dy=1), dev(dy=NY - 1), dev(dz=1), dev(dz=NZ - 1)
    row = [dev(dx=NX - j // NC, dc=NC - j % NC) for j in range(COLS)]
    order = (4, 5, 2, 3, 6, 7, 1)

    def remote(src, dst, s, r, to):
        return pltpu.make_async_remote_copy(
            src_ref=src, dst_ref=dst, send_sem=s, recv_sem=r, device_id=to, device_id_type=MESH
        )

    peers = [y_up, y_down, z_up, z_down, ahead, behind] + row[1:]
    barrier = pltpu.get_barrier_semaphore()
    for peer in peers:
        pl.semaphore_signal(barrier, inc=1, device_id=peer, device_id_type=MESH)

    in_copies = [
        pltpu.make_async_copy(src, dst, i_s.at[n])
        for n, (src, dst) in enumerate(((k_hbm, k_ref), (v_hbm, v_ref), (q_hbm, q_ref)))
    ]
    for copy in in_copies:
        copy.start()

    w_copies = []

    def w_begin():
        for h in range(HEADS):
            for k in range(NZ):
                at = ((z + Y_OF_K[k] + NZ) % NZ * HEADS + h) * DH
                src = w_ref.at[pl.ds(pl.multiple_of(at, DH), DH)]
                copy = pltpu.make_async_copy(src, w_bufs[h].at[pl.ds(k * DH, DH)], w_s.at[len(w_copies)])
                copy.start()
                w_copies.append(copy)

    in_copies[0].wait()
    pl.semaphore_wait(barrier, len(peers))

    def columns(sl):
        return pl.ds(DH if sl in (K1, V1) else 0, DH)

    def source(sl, blocks):
        return (k_ref if sl in (K0, K1) else v_ref).at[blocks, :, columns(sl)]

    def load(sl, k, off):
        if k:
            return y_bufs[sl][k - 1][off]
        return (k_ref if sl in (K0, K1) else v_ref)[off, :, columns(sl)]

    pending = []

    def start(copy):
        copy.start()
        pending.append(copy)

    def y_copy(sl, step, up, piece):
        blocks = pl.ds(*PIECES[piece])
        if step == 1:
            src = source(sl, blocks)
        else:
            src = y_bufs[sl][2 * step - (4 if up else 3)].at[blocks]
        dst = y_bufs[sl][6 if step == 4 else 2 * step - (2 if up else 1)].at[blocks]
        n = (step - 1) * 4 + (0 if up else 2) + piece
        return remote(src, dst, y_s.at[sl, n], y_r.at[sl, n], y_up if up else y_down)

    def moves(step, count=2):
        both = [(piece, up) for piece in range(count) for up in (True, False)]
        return both if step < 4 else [(piece, up) for piece, up in both if step == 4 and up == (2 * piece < count)]

    def y_begin(sl):
        for piece, up in moves(1):
            start(y_copy(sl, 1, up, piece))

    def y_step(sl, step):
        for piece, up in moves(step):
            y_copy(sl, step, up, piece).wait_recv()
            if (piece, up) in moves(step + 1):
                start(y_copy(sl, step + 1, up, piece))

    def x_step(sl, step):
        ks = STEP_KS[step]
        first, size = 2 * ks[0], 2 * len(ks)

        def fill(j, _):
            for k in ks:
                for slot in range(2):
                    stage[sl][(j - 1) * SLOTS + 2 * k + slot] = load(sl, k, send_t[j, 2 * k + slot])
            return 0

        lax.fori_loop(1, COLS, fill, 0)
        for j in order:
            remote(
                stage[sl].at[pl.ds((j - 1) * SLOTS + first, size)],
                land[sl].at[pl.ds(j * SLOTS + first, size)],
                x_s.at[sl],
                x_r.at[sl],
                row[j],
            ).start()
        for k in ks:
            for slot in range(2):
                land[sl][2 * k + slot] = load(sl, k, send_t[0, 2 * k + slot])

    def x_whole(sl):
        return remote(
            stage[sl].at[...], land[sl].at[pl.ds(SLOTS, (COLS - 1) * SLOTS)], x_s.at[sl], x_r.at[sl], row[1]
        )

    glob_at = []
    for g in range(G):
        block = glob[g]
        group = block // PER
        dy_g = (group // NC) % NY + NY - y
        dy_g = jnp.where(dy_g >= NY, dy_g - NY, dy_g)
        k_g = jnp.where(dy_g < 4, 2 * dy_g, jnp.where(dy_g == 4, 7, 15 - 2 * dy_g))
        dx_g = group // (NY * NC) + NX - x
        dx_g = jnp.where(dx_g >= NX, dx_g - NX, dx_g)
        glob_at.append((k_g, block % PER, dx_g, group % NC))

    def g_begin(sl):
        for g, (k_g, off, _, _) in enumerate(glob_at):
            block = load(sl, 0, off)
            for k in range(1, NY):
                block = jnp.where(k_g == k, load(sl, k, off), block)
            g_out[sl][g] = block
        for dx in (2, 1, 3):
            remote(g_out[sl], g_in[sl].at[pl.ds((dx - 1) * G, G)], g_s.at[sl], g_r.at[sl], row[dx * NC]).start()

    def g_whole(sl):
        return remote(g_in[sl], g_in[sl], g_s.at[sl], g_r.at[sl], row[NC])

    def g_cores(sl):
        return remote(g_sel[sl], g_other[sl], c_s.at[sl], c_r.at[sl], row[1])

    def g_mid(sl):
        g_whole(sl).wait_recv()
        for g, (_, _, dx_g, _) in enumerate(glob_at):
            block = g_out[sl][g]
            for dx in (1, 2, 3):
                block = jnp.where(dx_g == dx, g_in[sl][(dx - 1) * G + g], block)
            g_sel[sl][g] = block
        g_cores(sl).start()

    def g_end(sl):
        g_cores(sl).wait_recv()
        for g, (_, _, _, c_g) in enumerate(glob_at):
            g_fin[sl][g] = jnp.where(c_g == c, g_sel[sl][g], g_other[sl][g])

    halo = [[] for _ in range(4)]

    def edges(sl):
        for n, (src, dst, to) in enumerate(((PER - 1, 0, ahead), (0, PER + 1, behind))):
            copy = remote(source(sl, src), pads[sl].at[dst], h_s.at[sl, n], h_r.at[sl, n], to)
            copy.start()
            halo[sl].append(copy)

        def fill(i, _):
            pads[sl][i + 1] = load(sl, 0, i)
            return 0

        lax.fori_loop(0, PER, fill, 0)

    def ready(sl):
        for copy in halo[sl]:
            copy.wait_recv()
        x_whole(sl).wait_recv()
        g_end(sl)

    def gathered(sl, i):
        return (
            [pads[sl][i], pads[sl][i + 1], pads[sl][i + 2]]
            + [g_fin[sl][g] for g in range(G)]
            + [land[sl][read_t[0, n * 32 + i]] for n in range(R)]
        )

    def scores(h, begin, end):
        def one(i, _):
            blocks = gathered(K1 if h else K0, i)
            s = lax.dot_general(
                q_ref[i, :, pl.ds(h * DH, DH)],
                jnp.concatenate(blocks, axis=0),
                (((1,), (1,)), ((), ())),
                preferred_element_type=jnp.float32,
            )
            s = s * SCALE
            e = jnp.exp(s - jnp.max(s, axis=1, keepdims=True))
            t_bufs[h][i] = jnp.broadcast_to(jnp.sum(e, axis=1, keepdims=True), (BLOCK, DH))
            p_bufs[h][i] = e.astype(BF16)
            return 0

        lax.fori_loop(begin, end, one, 0)

    def context(h, begin, end):
        def one(i, _):
            blocks = gathered(V1 if h else V0, i)
            o = jnp.dot(p_bufs[h][i], jnp.concatenate(blocks, axis=0), preferred_element_type=jnp.float32)
            rows = pl.ds(pl.multiple_of(i * BLOCK, BLOCK), BLOCK)
            ctx[h][rows, pl.ds(0, DH)] = (o / t_bufs[h][i]).astype(BF16)
            return 0

        lax.fori_loop(begin, end, one, 0)

    def z_copy(t, step, up, piece):
        pieces = LAST_PIECES if t else PIECES
        first, size = pieces[piece]
        rows = pl.ds(first * BLOCK, size * BLOCK)
        from_k = 0 if step == 1 else 2 * step - (3 if up else 2)
        to_k = 7 if step == 4 else 2 * step - (1 if up else 0)
        n = (step - 1) * 8 + (0 if up else 4) + piece
        return remote(
            ctx[t].at[rows, pl.ds(from_k * DH, DH)],
            ctx[t].at[rows, pl.ds(to_k * DH, DH)],
            z_s.at[t, n],
            z_r.at[t, n],
            z_up if up else z_down,
        )

    def z_begin(t, piece):
        for up in (True, False):
            start(z_copy(t, 1, up, piece))

    def z_step(t, step, only=None):
        count = len(LAST_PIECES if t else PIECES)
        for piece, up in moves(step, count):
            if only is not None and piece not in only:
                continue
            z_copy(t, step, up, piece).wait_recv()
            if (piece, up) in moves(step + 1, count):
                start(z_copy(t, step + 1, up, piece))

    def project(h, k0, k1, begin=0, end=ROWS // TILE, first=False, last=False):
        cols = pl.ds(k0 * DH, (k1 - k0) * DH)

        def tile(n, _):
            rows = pl.ds(pl.multiple_of(n * TILE, 16), TILE)
            part = jnp.dot(ctx[h][rows, cols], w_bufs[h][cols, :], preferred_element_type=jnp.float32)
            if not first:
                part = part + acc[rows, :]
            if last:
                out_ref[rows, :] = part.astype(out_ref.dtype)
            else:
                acc[rows, :] = part
            return 0

        lax.fori_loop(begin, end, tile, 0)

    def tables():
        lane = lax.broadcasted_iota(jnp.int32, (COLS, DH), 1)

        def requests(holders):
            rs = [jnp.concatenate([code_ref[r, pl.ds(at, 1), :] for at in holders], axis=0) for r in range(R)]
            return jnp.where(lane < 32, rs[0], jnp.where(lane < 64, pltpu.roll(rs[1], 32, 1), pltpu.roll(rs[2], 64, 1)))

        asked = requests([row[j][0] for j in range(COLS)])
        ranked = lane * 32 + (asked & 31)
        asked = asked >> 5
        table = jnp.zeros((COLS, DH), jnp.int32)
        for k in range(NY):
            match = asked == dev(dy=Y_OF_K[k] + NY)[0]
            first = jnp.min(jnp.where(match, ranked, 1 << 12), axis=1, keepdims=True) & 31
            last = jnp.max(jnp.where(match, ranked, 0), axis=1, keepdims=True) & 31
            table = jnp.where(lane == 2 * k, first, jnp.where(lane == 2 * k + 1, last, table))
        send_v[...] = table
        mine = requests([seq] * COLS) >> 5
        rank = jnp.zeros((COLS, DH), jnp.int32)
        for d in range(1, 32 * (R - 1) + PER):
            rank = rank + jnp.where((pltpu.roll(mine, d, 1) == mine) & (lane >= d), 1, 0)
        column = (((mine >> 4) - x) & 3) * NC + (((mine & 1) - c) & 1)
        dy = (((mine >> 1) & 7) - y) & 7
        ring = jnp.where(dy < 4, 2 * dy, jnp.where(dy == 4, 7, 15 - 2 * dy))
        read_v[...] = column * SLOTS + 2 * ring + jnp.minimum(rank, 1)
        t_copies = [
            pltpu.make_async_copy(send_v, send_t, i_s.at[3]),
            pltpu.make_async_copy(read_v, read_t, i_s.at[4]),
        ]
        for copy in t_copies:
            copy.start()
        for copy in t_copies:
            copy.wait()

    y_begin(K0)
    tables()
    x_step(K0, 0)
    edges(K0)
    in_copies[1].wait()
    in_copies[2].wait()
    x_step(V0, 0)
    edges(V0)
    x_step(K1, 0)
    edges(K1)
    y_step(K0, 1)
    x_step(K0, 1)
    w_begin()
    edges(V1)
    y_step(K0, 2)
    y_begin(V0)
    x_step(K0, 2)
    x_step(V1, 0)
    y_step(K0, 3)
    x_step(K0, 3)
    y_step(V0, 1)
    x_step(V0, 1)
    y_step(K0, 4)
    g_begin(K0)
    x_step(K0, 4)
    y_step(V0, 2)
    y_begin(K1)
    x_step(V0, 2)
    g_mid(K0)
    y_step(V0, 3)
    x_step(V0, 3)
    ready(K0)
    scores(0, 0, 5)
    y_step(K1, 1)
    x_step(K1, 1)
    scores(0, 5, 9)
    y_step(V0, 4)
    g_begin(V0)
    x_step(V0, 4)
    scores(0, 9, 13)
    y_step(K1, 2)
    y_begin(V1)
    x_step(K1, 2)
    scores(0, 13, 17)
    g_mid(V0)
    y_step(K1, 3)
    x_step(K1, 3)
    ready(V0)
    context(0, 0, CUT)
    z_begin(0, 0)
    context(0, CUT, PER)
    z_begin(0, 1)
    y_step(V1, 1)
    x_step(V1, 1)
    y_step(K1, 4)
    g_begin(K1)
    x_step(K1, 4)
    z_step(0, 1)
    y_step(V1, 2)
    x_step(V1, 2)
    g_mid(K1)
    z_step(0, 2)
    y_step(V1, 3)
    x_step(V1, 3)
    ready(K1)
    scores(1, 0, 5)
    z_step(0, 3)
    y_step(V1, 4)
    g_begin(V1)
    x_step(V1, 4)
    scores(1, 5, 11)
    g_mid(V1)
    scores(1, 11, 17)
    z_step(0, 4)
    for copy in w_copies:
        copy.wait()
    ready(V1)
    for piece, (first, size) in enumerate(LAST_PIECES):
        context(1, first, first + size)
        z_begin(1, piece)
    project(0, 0, 8, 0, 2, first=True)
    z_step(1, 1)
    project(0, 0, 8, 2, 4, first=True)
    z_step(1, 2)
    project(1, 0, 5, 0, 2)
    z_step(1, 3, (0, 1))
    project(1, 0, 5, 2, 4)
    z_step(1, 3, (2, 3))
    project(1, 5, 7)
    z_step(1, 4)
    project(1, 7, 8, last=True)

    for copy in pending:
        copy.wait_send()
    for sl in range(4):
        for copy in halo[sl]:
            copy.wait_send()
        x_whole(sl).wait_send()
        g_whole(sl).wait_send()
        g_cores(sl).wait_send()


def on_device(queries, keys, values, rand_group, rand_offset, glob_blocks, w_out):
    n_seq = NX * NY * NC
    code = (rand_group * 32 + rand_offset).T.reshape(R, n_seq, PER)
    code = jnp.pad(code, ((0, 0), (0, 0), (0, DH - PER)), constant_values=-1)
    shape = (PER, BLOCK, HEADS * DH)
    features = w_out.shape[1]
    vmem = pltpu.VMEM

    def per_slice(blocks):
        return [vmem((blocks, BLOCK, DH), BF16)] * 4

    scratch = [vmem(shape, BF16)] * 3 + [vmem((COLS, DH), jnp.int32)] * 2 + [pltpu.SMEM((COLS, DH), jnp.int32)] * 2
    scratch += per_slice(PER) * (NY - 1)
    for blocks in ((COLS - 1) * SLOTS, COLS * SLOTS, PER + 2, G, 3 * G, G, G, G):
        scratch += per_slice(blocks)
    scratch += [vmem((PER, BLOCK, KEYS), BF16)] * 2
    scratch += [vmem((PER, BLOCK, DH), jnp.float32)] * 2
    scratch += [vmem((ROWS, NZ * DH), BF16)] * 2
    scratch += [vmem((NZ * DH, features), BF16)] * 2
    scratch += [vmem((ROWS, features), jnp.float32)]
    dma = pltpu.SemaphoreType.DMA
    scratch += [dma((4, 16)), dma((4, 16))] + [dma((4,))] * 6 + [dma((4, 2))] * 2
    scratch += [dma((2, 32)), dma((2, 32)), dma((HEADS * NZ,)), dma((5,))]
    hbm = pl.BlockSpec(memory_space=pl.ANY)
    whole = pl.BlockSpec(memory_space=vmem)
    return pl.pallas_call(
        kernel,
        out_shape=jax.ShapeDtypeStruct((ROWS, features), BF16),
        in_specs=[pl.BlockSpec(memory_space=pltpu.SMEM), whole, hbm, hbm, hbm, hbm],
        out_specs=whole,
        scratch_shapes=scratch,
        compiler_params=pltpu.CompilerParams(collective_id=0, has_side_effects=True, vmem_limit_bytes=60 << 20),
        name="sparse_attention",
    )(glob_blocks, code, queries.reshape(shape), keys.reshape(shape), values.reshape(shape), w_out)


def solution(mesh):
    return jax.shard_map(
        on_device,
        mesh=mesh,
        in_specs=(P("seq", "head"), P("seq", "head"), P("seq", "head"), P(), P(), P(), P(None, "head")),
        out_specs=P("seq", "head"),
        check_vma=False,
    )
```
